32 devices in a mesh: groups: 2 (over y), seg: 4 (over z), section: 4 (over x, core).
Axes of the slice: x: 2, y: 2, z: 4, core: 2. Of those that a mesh axis runs over, the one named last changes fastest.
Arguments:
- writes: bfloat16 [8, 128, 2048], P(('groups', 'seg'), None, 'section'), parts along dimension 0, may hold values from -6 to 6
- layer_inputs: bfloat16 [4, 8, 256, 2048], P('section', ('groups', 'seg')), parts along dimension 1, may hold values from -6 to 6
- upstream: bfloat16 [4, 8, 256, 2048], P('section', ('groups', 'seg')), parts along dimension 1, may hold values from -6 to 6
- pattern: int32 [8, 2, 3], P(('groups', 'seg')), parts along dimension 0, may hold values 0 or 1
- w_q: bfloat16 [4, 2048, 1024], P('section', 'seg'), may hold values from -0.125 to 0.125
- w_kv: bfloat16 [4, 2048, 512], P('section', 'seg'), may hold values from -0.125 to 0.125
- w_o: bfloat16 [4, 1024, 2048], P('section', 'seg'), may hold values from -0.1875 to 0.1875
- norm_gain: float32 [4, 2048], P('section'), may hold values from 0.5 to 10
- gate_weight: float32 [4, 2048, 16], P('section'), may hold values from -0.125 to 0.125
- gate_bias: float32 [4, 16], P('section'), may hold values from -2 to 6
Outputs:
- section_grads: bfloat16 [4, 8, 256, 2048], P('section', ('groups', 'seg')), parts along dimension 1
- memory_grads: bfloat16 [4, 8, 128, 2048], P('section', ('groups', 'seg')), parts along dimension 1
The draws below stay inside these ranges and needn't reach their ends.
There are 2 independent parts, one for each index of `groups`. The reference program is written for one: setup_inputs(seed, part) draws one part's arguments, and reference() takes and returns one part's arrays. A program takes and returns all parts, laid end to end along the dimension named above; an argument that names none is the same for every part. Nothing has to cross between parts.
All inputs are finite; a program needn't handle non-finite values. No bound on the sum of `pattern` on one device may be relied on, other than what follows from the above.
Results may differ from the reference program's by a relative error of at most 0.03.
The reference program's roundings to bfloat16 on the way count: a program that leaves them out, or rounds other values in their place, can miss the bound.
Values may be sent and summed in bfloat16 or wider, within the bound.
A program may use at most 128 MiB of HBM per device.

```python
import jax
import jax.numpy as jnp
from jax import lax

D = 2048
HEADS = 16
KV_HEADS = 4
HEAD = 64
BLK = 128
MEM = 128
SEG_LEN = 256
SEGMENTS = 4
N_SECTION = 4


def draw_norm_gain(key, part):
    values = jnp.clip(1.0 + 0.1 * jax.random.normal(key, (N_SECTION, D), jnp.float32), 0.5, 1.5)
    return values


def with_ends(values, rng, least, high):
    longest = values.shape.index(max(values.shape))
    spots = []
    for shift in (0, 1):
        where = [jax.random.randint(jax.random.fold_in(rng, axis), (), 0, length) for axis, length in enumerate(values.shape)]
        where[longest] = (where[longest] + shift) % values.shape[longest]
        spots.append(tuple(where))
    return values.at[spots[0]].set(least).at[spots[1]].set(high)


def block_levels(rng, dims, pieces, least, high):
    level, own = 1.0, jax.random.fold_in(rng, 6)
    for axis_at, blocks in pieces:
        heights = jnp.exp(jax.random.uniform(jax.random.fold_in(own, axis_at), (blocks,), jnp.float32, least / len(pieces), high / len(pieces)))
        level = level * jnp.repeat(heights, dims[axis_at] // blocks).reshape([-1 if axis == axis_at else 1 for axis in range(len(dims))])
    return level


def bell_draw(key, dims, deviation, bound, split=(), kind=jnp.bfloat16):
    array = deviation * jax.random.normal(key, dims, jnp.float32)
    if split:
        array = array * block_levels(key, dims, split, -0.22, 0.18)
    return jnp.clip(array, -bound, bound).astype(kind)


def setup_inputs(seed: int = 0, part: int = 0) -> dict:
    arg_keys = jax.random.split(jax.random.key(seed), 11)
    own_keys = jax.random.split(jax.random.fold_in(arg_keys[10], part), 11)
    return {
        "writes": bell_draw(own_keys[0], (SEGMENTS, MEM, D), 1.0, 6.0, ((0, 4), (2, 4))),
        "layer_inputs": bell_draw(own_keys[1], (N_SECTION, SEGMENTS, SEG_LEN, D), 1.0, 6.0, ((0, 4), (1, 4))),
        "upstream": bell_draw(own_keys[2], (N_SECTION, SEGMENTS, SEG_LEN, D), 1.0, 6.0, ((0, 4), (1, 4))),
        "pattern": with_ends((jax.random.randint(own_keys[3], (SEGMENTS, SEG_LEN // BLK, SEG_LEN // BLK + 1), 0, 2) < 1).astype(jnp.int32), jax.random.fold_in(own_keys[3], 1), 0, 1),
        "w_q": bell_draw(arg_keys[4], (N_SECTION, D, HEADS * HEAD), D ** -0.5, 0.125, ((0, 4), (1, 4))),
        "w_kv": bell_draw(arg_keys[5], (N_SECTION, D, 2 * KV_HEADS * HEAD), D ** -0.5, 0.125, ((0, 4), (1, 4))),
        "w_o": bell_draw(arg_keys[6], (N_SECTION, HEADS * HEAD, D), (HEADS * HEAD) ** -0.5, 0.1875, ((0, 4), (1, 4))),
        "norm_gain": draw_norm_gain(jax.random.fold_in(arg_keys[10], 71), part),
        "gate_weight": bell_draw(arg_keys[8], (N_SECTION, D, HEADS), D ** -0.5, 0.125, ((0, 4),), jnp.float32),
        "gate_bias": jnp.clip(-2.0 + 8.0 * jax.random.uniform(arg_keys[9], (N_SECTION, HEADS), jnp.float32) ** block_levels(arg_keys[9], (N_SECTION, HEADS), ((0, 4),), -0.2, 0.2), -2.0, 6.0),
    }


epsilon = 1e-05
masked_score = -1e+30

def normed_rows(values, gain):
    widened = values.astype(jnp.float32)
    scale = lax.rsqrt(lax.optimization_barrier(jnp.mean(widened * widened, axis=-1, keepdims=True)) + epsilon)
    return (widened * scale * gain).astype(jnp.bfloat16)

def allowed_keys(positions, layout, block_rows, memory_rows, total_rows):
    blocks = layout.shape[0]
    query_block = positions // block_rows
    chooser = (query_block[:, None] == jnp.arange(blocks, dtype=jnp.int32)[None, :]).astype(jnp.int32)
    picked = lax.optimization_barrier(jnp.sum(chooser[:, :, None] * layout[None, :, :], axis=1))
    token_index = jnp.arange(total_rows, dtype=jnp.int32)
    key_block = token_index // block_rows
    spread = (key_block[None, :] == jnp.arange(blocks, dtype=jnp.int32)[:, None]).astype(jnp.int32)
    token_pattern = lax.optimization_barrier(jnp.sum(picked[:, 1:, None] * spread[None, :, :], axis=1))
    earlier = (key_block[None, :] < query_block[:, None]) & (token_pattern > 0)
    causal = (key_block[None, :] == query_block[:, None]) & (token_index[None, :] <= positions[:, None])
    memory_part = jnp.broadcast_to((picked[:, 0] > 0)[:, None], (positions.shape[0], memory_rows))
    return jnp.concatenate([memory_part, earlier | causal], axis=1)

def attend_rows(queries, keyvals, allowed):
    count = queries.shape[0]
    sources = keyvals.shape[0]
    grouped = queries.astype(jnp.float32).reshape(count, KV_HEADS, HEADS // KV_HEADS, HEAD)
    keys = keyvals[:, :KV_HEADS * HEAD].astype(jnp.float32).reshape(sources, KV_HEADS, HEAD)
    values = keyvals[:, KV_HEADS * HEAD:].astype(jnp.float32).reshape(sources, KV_HEADS, HEAD)
    scores = jnp.einsum('qgre,sge->grqs', grouped, keys) * HEAD ** (-0.5)
    scores = jnp.where(allowed[None, None], scores, masked_score)
    peak = lax.stop_gradient(lax.optimization_barrier(jnp.max(scores, axis=-1, keepdims=True)))
    weights = jnp.exp(scores - peak)
    probs = (weights / lax.optimization_barrier(jnp.sum(weights, axis=-1, keepdims=True))).astype(jnp.bfloat16)
    mixed = jnp.einsum('grqs,sge->qgre', probs.astype(jnp.float32), values)
    return mixed.reshape(count, HEADS * HEAD).astype(jnp.bfloat16)

def apply_layer(stream, memory, layout, query_weight, pair_weight, out_weight, gain):
    memory_rows = memory.shape[0]
    count = stream.shape[0]
    normed = normed_rows(jnp.concatenate([memory, stream], axis=0), gain)
    queries = jnp.dot(normed[memory_rows:], query_weight, preferred_element_type=jnp.float32).astype(jnp.bfloat16)
    keyvals = jnp.dot(normed, pair_weight, preferred_element_type=jnp.float32).astype(jnp.bfloat16)
    positions = jnp.arange(count, dtype=jnp.int32)
    allowed = allowed_keys(positions, layout, BLK, memory_rows, count)
    mixed = attend_rows(queries, keyvals, allowed)
    added = jnp.dot(mixed, out_weight, preferred_element_type=jnp.float32)
    return (stream.astype(jnp.float32) + added).astype(jnp.bfloat16)

def memory_states(writes, gate_weight, gate_bias):
    widened = writes.astype(jnp.float32)
    logits = jnp.einsum('smd,dg->smg', widened, gate_weight, precision=lax.Precision.HIGHEST) + gate_bias
    keep = jax.nn.sigmoid(logits)
    segments, rows, width = widened.shape
    grouped = widened.reshape(segments, rows, HEADS, width // HEADS)

    def advance(state, item):
        keep_now, write_now = item
        following = keep_now[:, :, None] * state + (1.0 - keep_now)[:, :, None] * write_now
        return (following, state)
    start = jnp.zeros((rows, HEADS, width // HEADS), jnp.float32)
    _, states = lax.scan(advance, start, (keep, grouped))
    return states.reshape(segments, rows, width).astype(jnp.bfloat16)

def reference(writes, layer_inputs, upstream, pattern, w_q, w_kv, w_o, norm_gain, gate_weight, gate_bias):
    section_list = []
    memory_list = []
    for level in range(N_SECTION):
        memory = memory_states(writes, gate_weight[level], gate_bias[level])

        def backward_one(item, level=level):
            rows_in, memory_in, layout, incoming = item

            def mapping(first_arg, second_arg):
                return apply_layer(first_arg, second_arg, layout, w_q[level], w_kv[level], w_o[level], norm_gain[level])
            _, pull = jax.vjp(mapping, rows_in, memory_in)
            return pull(incoming)
        grad_rows, grad_memory = lax.map(backward_one, (layer_inputs[level], memory, pattern, upstream[level]))
        section_list.append(grad_rows.astype(jnp.bfloat16))
        memory_list.append(grad_memory.astype(jnp.bfloat16))
    return (jnp.stack(section_list), jnp.stack(memory_list))
```

```python
import functools

import jax
import jax.numpy as jnp
from jax import lax
from jax.experimental import pallas as pl
from jax.experimental.pallas import tpu as pltpu
from jax.sharding import PartitionSpec as P

HEADS = 16
KV_HEADS = 4
HEAD = 64
BLK = 128
MEM = 128


epsilon = 1e-05
masked_score = -1e30


def gather_kernel(
    n, groups, sections, writes, w_kv, w_q, w_o, all_writes, all_kv, all_q, all_o, *sems
):
    up_sem, down_sem, zrecv, ysend, yrecv, wsend, wrecv, psend, precv, local = sems
    g = lax.axis_index("groups")
    s = lax.axis_index("seg")
    c = lax.axis_index("section")
    weights = ((w_kv, all_kv), (w_q, all_q), (w_o, all_o))
    wide = writes.shape[1]
    mine = pl.ds(pl.multiple_of(c * wide, wide), wide)

    barrier = pltpu.get_barrier_semaphore()

    def greet(where):
        pl.semaphore_signal(
            barrier, inc=1, device_id=where, device_id_type=pl.DeviceIdType.MESH
        )

    @pl.when(s > 0)
    def _():
        greet((g, s - 1, c))

    @pl.when(s < n - 1)
    def _():
        greet((g, s + 1, c))

    for d in range(1, groups):
        greet(((g + d) % groups, s, c))
    for d in range(1, sections):
        greet((g, s, (c + d) % sections))

    beside = (s + n - 1) // n + (2 * n - 2 - s) // n
    pl.semaphore_wait(barrier, beside + groups + sections - 2)

    def remote(src, dst, send, recv, where):
        return pltpu.make_async_remote_copy(
            src_ref=src,
            dst_ref=dst,
            send_sem=send,
            recv_sem=recv,
            device_id=where,
            device_id_type=pl.DeviceIdType.MESH,
        )

    def up(i, shard, own=False):
        src, dst = weights[i]
        spot = dst.at[shard, g]
        return remote(
            src.at[g] if own else spot, spot, up_sem.at[i, shard], zrecv.at[i, shard], (g, s + 1, c)
        )

    def down(i, shard, own=False):
        src, dst = weights[i]
        spot = dst.at[shard, g]
        return remote(
            src.at[g] if own else spot, spot, down_sem.at[i, shard], zrecv.at[i, shard], (g, s - 1, c)
        )

    def across(i, shard, d):
        spot = weights[i][1].at[shard, g]
        return remote(
            spot, spot, ysend.at[i, shard, d], yrecv.at[i, shard, d], ((g + d) % groups, s, c)
        )

    def across_in(i, shard, d):
        spot = weights[i][1].at[shard, (g + groups - d) % groups]
        return remote(
            spot, spot, ysend.at[i, shard, d], yrecv.at[i, shard, d], ((g + d) % groups, s, c)
        )

    def write_up(shard, own=False):
        spot = all_writes.at[shard, :, mine]
        return remote(
            writes if own else spot, spot, wsend.at[shard], wrecv.at[shard], (g, s + 1, c)
        )

    def write_peer(shard, d):
        spot = all_writes.at[shard, :, mine]
        return remote(
            spot, spot, psend.at[shard, d], precv.at[shard, d], (g, s, (c + d) % sections)
        )

    def write_peer_in(shard, d):
        origin = (c + sections - d) % sections
        spot = all_writes.at[shard, :, pl.ds(pl.multiple_of(origin * wide, wide), wide)]
        return remote(
            spot, spot, psend.at[shard, d], precv.at[shard, d], (g, s, (c + d) % sections)
        )

    def own_copy(i):
        src, dst = weights[i]
        return pltpu.make_async_copy(src, dst.at[s], local.at[i])

    def start_own(i):
        @pl.when(s < n - 1)
        def _():
            up(i, s, True).start()

        @pl.when(s > 0)
        def _():
            down(i, s, True).start()

        own_copy(i).start()

    @pl.when(s < n - 1)
    def _():
        write_up(s, True).start()

    start_own(0)

    @pl.loop(1, n)
    def _(k):
        @pl.when(s - k >= 0)
        def _():
            write_up(s - k).wait_recv()

            @pl.when(s < n - 1)
            def _():
                write_up(s - k).start()

            for d in range(1, sections):
                write_peer(s - k, d).start()

    for i in range(len(weights)):
        if i + 1 < len(weights):
            start_own(i + 1)

        @pl.loop(1, n)
        def _(k, i=i):
            @pl.when(s - k >= 0)
            def _():
                up(i, s - k).wait_recv()

                @pl.when(s < n - 1)
                def _():
                    up(i, s - k).start()

                for d in range(1, groups):
                    across(i, s - k, d).start()

            @pl.when(s + k < n)
            def _():
                down(i, s + k).wait_recv()

                @pl.when(s > 0)
                def _():
                    down(i, s + k).start()

                for d in range(1, groups):
                    across(i, s + k, d).start()

    @pl.loop(0, n)
    def _(shard):
        @pl.when(shard < s)
        def _():
            for d in range(1, sections):
                write_peer_in(shard, d).wait_recv()
                write_peer(shard, d).wait_send()

        @pl.when((shard <= s) & (s < n - 1))
        def _():
            write_up(shard).wait_send()

    for i in range(len(weights)):

        @pl.loop(0, n)
        def _(shard, i=i):
            @pl.when(shard != s)
            def _():
                for d in range(1, groups):
                    across_in(i, shard, d).wait_recv()
                    across(i, shard, d).wait_send()

            @pl.when((shard <= s) & (s < n - 1))
            def _():
                up(i, shard).wait_send()

            @pl.when((shard >= s) & (s > 0))
            def _():
                down(i, shard).wait_send()

        own_copy(i).wait()


def gather_all(n, groups, sections, writes, w_kv, w_q, w_o):
    def halves(w):
        return w.reshape(groups, w.shape[0] // groups, w.shape[1])

    shards = [halves(w) for w in (w_kv, w_q, w_o)]
    rows, wide = writes.shape
    anywhere = pl.BlockSpec(memory_space=pl.ANY)
    dma = pltpu.SemaphoreType.DMA
    outs = pl.pallas_call(
        functools.partial(gather_kernel, n, groups, sections),
        out_shape=[jax.ShapeDtypeStruct((n, rows, wide * sections), writes.dtype)]
        + [jax.ShapeDtypeStruct((n, *w.shape), w.dtype) for w in shards],
        in_specs=[anywhere] * 4,
        out_specs=[anywhere] * 4,
        scratch_shapes=[
            dma((3, n)),
            dma((3, n)),
            dma((3, n)),
            dma((3, n, groups)),
            dma((3, n, groups)),
            dma((n,)),
            dma((n,)),
            dma((n, sections)),
            dma((n, sections)),
            dma((3,)),
        ],
        compiler_params=pltpu.CompilerParams(collective_id=0, has_side_effects=True),
    )(writes, *shards)
    full = [w.reshape(-1, w.shape[-1]) for w in outs[1:]]
    return outs[0], *full


def normed_rows(values, gain):
    widened = values.astype(jnp.float32)
    scale = lax.rsqrt(jnp.mean(widened * widened, axis=-1, keepdims=True) + epsilon)
    return (widened * scale * gain).astype(jnp.bfloat16)


def allowed_keys(positions, layout, block_rows, memory_rows, total_rows):
    blocks = layout.shape[0]
    query_block = positions // block_rows
    chooser = (query_block[:, None] == jnp.arange(blocks, dtype=jnp.int32)[None, :]).astype(
        jnp.int32
    )
    picked = jnp.sum(chooser[:, :, None] * layout[None, :, :], axis=1)
    token_index = jnp.arange(total_rows, dtype=jnp.int32)
    key_block = token_index // block_rows
    spread = (key_block[None, :] == jnp.arange(blocks, dtype=jnp.int32)[:, None]).astype(jnp.int32)
    token_pattern = jnp.sum(picked[:, 1:, None] * spread[None, :, :], axis=1)
    earlier = (key_block[None, :] < query_block[:, None]) & (token_pattern > 0)
    causal = (key_block[None, :] == query_block[:, None]) & (
        token_index[None, :] <= positions[:, None]
    )
    memory_part = jnp.broadcast_to((picked[:, 0] > 0)[:, None], (positions.shape[0], memory_rows))
    return jnp.concatenate([memory_part, earlier | causal], axis=1)


def attend_rows(queries, keyvals, allowed):
    count = queries.shape[0]
    sources = keyvals.shape[0]
    grouped = queries.reshape(count, KV_HEADS, HEADS // KV_HEADS, HEAD)
    keys = keyvals[:, : KV_HEADS * HEAD].reshape(sources, KV_HEADS, HEAD)
    values = keyvals[:, KV_HEADS * HEAD :].reshape(sources, KV_HEADS, HEAD)
    scores = jnp.einsum(
        "qgre,sge->grqs", grouped, keys, preferred_element_type=jnp.float32
    ) * HEAD ** (-0.5)
    scores = jnp.where(allowed[None, None], scores, masked_score)
    peak = lax.stop_gradient(jnp.max(scores, axis=-1, keepdims=True))
    weights = jnp.exp(scores - peak)
    probs = (weights / jnp.sum(weights, axis=-1, keepdims=True)).astype(jnp.bfloat16)
    mixed = jnp.einsum("grqs,sge->qgre", probs, values, preferred_element_type=jnp.float32)
    return mixed.reshape(count, HEADS * HEAD).astype(jnp.bfloat16)


def apply_layer(stream, memory, layout, query_weight, pair_weight, out_weight, gain):
    memory_rows = memory.shape[0]
    count = stream.shape[0]
    normed = normed_rows(jnp.concatenate([memory, stream], axis=0), gain)
    queries = jnp.dot(
        normed[memory_rows:], query_weight, preferred_element_type=jnp.float32
    ).astype(jnp.bfloat16)
    keyvals = jnp.dot(normed, pair_weight, preferred_element_type=jnp.float32).astype(jnp.bfloat16)
    positions = jnp.arange(count, dtype=jnp.int32)
    allowed = allowed_keys(positions, layout, BLK, memory_rows, count)
    mixed = attend_rows(queries, keyvals, allowed)
    added = jnp.dot(mixed, out_weight, preferred_element_type=jnp.float32)
    return (stream.astype(jnp.float32) + added).astype(jnp.bfloat16)


def per_device(
    n,
    groups,
    sections,
    writes,
    layer_inputs,
    upstream,
    pattern,
    w_q,
    w_kv,
    w_o,
    norm_gain,
    gate_weight,
    gate_bias,
):
    all_writes, pair_weight, query_weight, out_weight = gather_all(
        n, groups, sections, writes[0], w_kv[0], w_q[0], w_o[0]
    )
    rows_in = layer_inputs[0, 0]
    incoming = upstream[0, 0]
    layout = pattern[0]
    gain = norm_gain[0]
    width = rows_in.shape[1]
    place = lax.axis_index("seg")
    earlier = jnp.arange(n) < place
    widened = jnp.where(earlier[:, None, None], all_writes, 0).astype(jnp.float32)
    logits = (
        jnp.dot(
            widened.reshape(n * MEM, width), gate_weight[0], precision=lax.Precision.HIGHEST
        )
        + gate_bias[0]
    )
    keep = jax.nn.sigmoid(logits).reshape(n, MEM, HEADS)

    def advance(at, state):
        share = keep[at][:, :, None]
        fresh = widened[at].reshape(MEM, HEADS, width // HEADS)
        return jnp.where(at < place, share * state + (1.0 - share) * fresh, state)

    state = lax.fori_loop(
        0, n, advance, jnp.zeros((MEM, HEADS, width // HEADS), jnp.float32), unroll=n <= 8
    )
    memory = state.reshape(MEM, width).astype(jnp.bfloat16)

    def mapping(first_arg, second_arg):
        return apply_layer(
            first_arg, second_arg, layout, query_weight, pair_weight, out_weight, gain
        )

    _, pull = jax.vjp(mapping, rows_in, memory)
    grad_rows, grad_memory = pull(incoming)
    return (grad_rows[None, None], grad_memory[None, None])


def solution(mesh):
    placed = (
        P(("groups", "seg"), None, "section"),
        P("section", ("groups", "seg"), None, None),
        P("section", ("groups", "seg"), None, None),
        P(("groups", "seg"), None, None),
        P("section", "seg", None),
        P("section", "seg", None),
        P("section", "seg", None),
        P("section", None),
        P("section", None, None),
        P("section", None),
    )
    sizes = (mesh.shape["seg"], mesh.shape["groups"], mesh.shape["section"])
    return jax.shard_map(
        functools.partial(per_device, *sizes),
        mesh=mesh,
        in_specs=placed,
        out_specs=(
            P("section", ("groups", "seg"), None, None),
            P("section", ("groups", "seg"), None, None),
        ),
        check_vma=False,
    )
```

```python
import functools

import jax
import jax.numpy as jnp
from jax import lax
from jax.experimental import pallas as pl
from jax.experimental.pallas import tpu as pltpu
from jax.sharding import PartitionSpec as P

HEADS = 16
KV_HEADS = 4
HEAD = 64
BLK = 128
MEM = 128


epsilon = 1e-05
masked_score = -1e30
GROUP = HEADS // KV_HEADS
NT = (((1,), (1,)), ((), ()))
TN = (((0,), (0,)), ((), ()))
CHUNKS = KV_HEADS


def layer_kernel(
    n,
    groups,
    sections,
    pattern,
    writes,
    rows_in,
    upstream,
    gain,
    gate,
    gate_bias,
    w_kv,
    w_q,
    w_o,
    grad_rows,
    grad_memory,
    all_writes,
    all_kv,
    all_q,
    all_o,
    normed,
    scales,
    memory,
    state,
    gates,
    keys,
    values,
    bias,
    dmixed,
    dq,
    dkeys,
    dvalues,
    dnormed,
    *sems,
):
    up_sem, down_sem, zrecv, ysend, yrecv, wsend, wrecv, psend, precv, local = sems
    g = lax.axis_index("groups")
    s = lax.axis_index("seg")
    c = lax.axis_index("section")
    count, width = rows_in.shape
    wide = writes.shape[1]
    span = all_q.shape[1] // CHUNKS
    f32, bf16 = jnp.float32, jnp.bfloat16

    def lanes(at, size):
        return pl.ds(pl.multiple_of(at * size, size), size)

    mine = lanes(c, wide)
    weights = ((w_kv, all_kv), (w_o, all_o), (w_q, all_q))

    barrier = pltpu.get_barrier_semaphore()

    def greet(where):
        pl.semaphore_signal(
            barrier, inc=1, device_id=where, device_id_type=pl.DeviceIdType.MESH
        )

    @pl.when(s > 0)
    def _():
        greet((g, s - 1, c))

    @pl.when(s < n - 1)
    def _():
        greet((g, s + 1, c))

    for d in range(1, groups):
        greet(((g + d) % groups, s, c))
    for d in range(1, sections):
        greet((g, s, (c + d) % sections))

    beside = (s + n - 1) // n + (2 * n - 2 - s) // n
    pl.semaphore_wait(barrier, beside + groups + sections - 2)

    def remote(src, dst, send, recv, where):
        return pltpu.make_async_remote_copy(
            src_ref=src,
            dst_ref=dst,
            send_sem=send,
            recv_sem=recv,
            device_id=where,
            device_id_type=pl.DeviceIdType.MESH,
        )

    def spot(item, shard, part):
        w, chunk = item
        src, dst = weights[w]
        half = src.shape[0] // groups
        rows = pl.ds(pl.multiple_of((shard * groups + part) * half, half), half)
        return dst.at[rows, :] if chunk is None else dst.at[rows, lanes(chunk, span)]

    def source(item):
        w, chunk = item
        src, _ = weights[w]
        half = src.shape[0] // groups
        rows = lanes(g, half)
        return src.at[rows, :] if chunk is None else src.at[rows, lanes(chunk, span)]

    def index(item):
        w, chunk = item
        return w if chunk is None else w + chunk

    def up(item, shard, own=False):
        i, there = index(item), spot(item, shard, g)
        src = source(item) if own else there
        return remote(src, there, up_sem.at[i, shard], zrecv.at[i, shard], (g, s + 1, c))

    def down(item, shard, own=False):
        i, there = index(item), spot(item, shard, g)
        src = source(item) if own else there
        return remote(src, there, down_sem.at[i, shard], zrecv.at[i, shard], (g, s - 1, c))

    def across(item, shard, d, part):
        i, there = index(item), spot(item, shard, part)
        return remote(
            there, there, ysend.at[i, shard, d], yrecv.at[i, shard, d], ((g + d) % groups, s, c)
        )

    def write_up(shard, own=False):
        there = all_writes.at[shard, :, mine]
        return remote(
            writes if own else there, there, wsend.at[shard], wrecv.at[shard], (g, s + 1, c)
        )

    def write_peer(shard, d, origin):
        there = all_writes.at[shard, :, lanes(origin, wide)]
        return remote(
            there, there, psend.at[shard, d], precv.at[shard, d], (g, s, (c + d) % sections)
        )

    def own_copy(w):
        src, dst = weights[w]
        return pltpu.make_async_copy(src, dst.at[lanes(s, src.shape[0]), :], local.at[w])

    def start_own(item):
        @pl.when(s < n - 1)
        def _():
            up(item, s, True).start()

        @pl.when(s > 0)
        def _():
            down(item, s, True).start()

    def service(item):
        @pl.loop(1, n)
        def _(k):
            @pl.when(s - k >= 0)
            def _():
                up(item, s - k).wait_recv()

                @pl.when(s < n - 1)
                def _():
                    up(item, s - k).start()

                for d in range(1, groups):
                    across(item, s - k, d, g).start()

            @pl.when(s + k < n)
            def _():
                down(item, s + k).wait_recv()

                @pl.when(s > 0)
                def _():
                    down(item, s + k).start()

                for d in range(1, groups):
                    across(item, s + k, d, g).start()

    def finish(item):
        @pl.loop(0, n)
        def _(shard):
            @pl.when(shard != s)
            def _():
                for d in range(1, groups):
                    across(item, shard, d, (g + groups - d) % groups).wait_recv()

    def drain(item):
        @pl.loop(0, n)
        def _(shard):
            @pl.when(shard != s)
            def _():
                for d in range(1, groups):
                    across(item, shard, d, g).wait_send()

            @pl.when((shard <= s) & (s < n - 1))
            def _():
                up(item, shard).wait_send()

            @pl.when((shard >= s) & (s > 0))
            def _():
                down(item, shard).wait_send()

    kv_item, o_item = (0, None), (1, None)

    def q_item(chunk):
        return (2, chunk)

    @pl.when(s < n - 1)
    def _():
        write_up(s, True).start()

    start_own(kv_item)
    start_own(o_item)
    for w in range(3):
        own_copy(w).start()

    strip = 32

    def norm_rows(from_ref, to_row):
        @pl.loop(0, from_ref.shape[0] // strip)
        def _(r):
            x = from_ref[lanes(r, strip), :].astype(f32)
            scale = lax.rsqrt(jnp.mean(x * x, axis=-1, keepdims=True) + epsilon)
            to = pl.ds(pl.multiple_of(to_row + r * strip, strip), strip)
            normed[to, :] = (x * scale * gain[...]).astype(bf16)
            scales[to, :] = scale

    norm_rows(rows_in, MEM)

    whole_gate = gate[...]
    high = whole_gate.astype(bf16)
    rest = whole_gate - high.astype(f32)
    middle = rest.astype(bf16)
    gates[0] = high
    gates[1] = middle
    gates[2] = (rest - middle.astype(f32)).astype(bf16)

    keyed = lax.broadcasted_iota(jnp.int32, (BLK, BLK), 0)
    asked = lax.broadcasted_iota(jnp.int32, (BLK, BLK), 1)
    blocks = count // BLK
    for b in range(blocks):
        to = slice(b * BLK, (b + 1) * BLK)
        seen = jnp.where(pattern[b, 0] > 0, 0.0, masked_score)
        bias[:MEM, to] = jnp.full((MEM, BLK), seen, f32)
        for e in range(blocks):
            where = slice(MEM + e * BLK, MEM + (e + 1) * BLK)
            if e == b:
                bias[where, to] = jnp.where(keyed <= asked, 0.0, masked_score).astype(f32)
            elif e < b:
                seen = jnp.where(pattern[b, 1 + e] > 0, 0.0, masked_score)
                bias[where, to] = jnp.full((BLK, BLK), seen, f32)
            else:
                bias[where, to] = jnp.full((BLK, BLK), masked_score, f32)

    @pl.loop(1, n)
    def _(k):
        @pl.when(s - k >= 0)
        def _():
            write_up(s - k).wait_recv()

            @pl.when(s < n - 1)
            def _():
                write_up(s - k).start()

            for d in range(1, sections):
                write_peer(s - k, d, c).start()

    service(kv_item)
    start_own(q_item(0))
    start_own(q_item(1))

    state[...] = jnp.zeros_like(state)
    cut = width // HEADS

    @pl.loop(0, n)
    def _(k):
        @pl.when(k < s)
        def _():
            for d in range(1, sections):
                write_peer(k, d, (c + sections - d) % sections).wait_recv()
            w = all_writes[k]
            logits = sum(jnp.dot(w, gates[p], preferred_element_type=f32) for p in range(3))
            keep = jax.nn.sigmoid(logits + gate_bias[...])
            for h in range(HEADS):
                at = slice(h * cut, (h + 1) * cut)
                share = keep[:, h : h + 1]
                state[:, at] = share * state[:, at] + (1.0 - share) * w[:, at].astype(f32)

    memory[...] = state[...].astype(bf16)
    norm_rows(memory, 0)

    service(o_item)
    start_own(q_item(2))
    start_own(q_item(3))

    own_copy(0).wait()
    finish(kv_item)
    for kind, to in ((0, keys), (1, values)):
        part = jnp.dot(
            normed[...], all_kv[:, kind * span : (kind + 1) * span], preferred_element_type=f32
        ).astype(bf16)
        for h in range(KV_HEADS):
            to[h] = part[:, h * HEAD : (h + 1) * HEAD]

    service(q_item(0))

    own_copy(1).wait()
    finish(o_item)

    @pl.loop(0, KV_HEADS)
    def _(j):
        dmixed[j] = lax.dot_general(
            upstream[...], all_o[lanes(j, span), :], NT, preferred_element_type=f32
        ).astype(bf16)

    own_copy(2).wait()

    @pl.loop(0, KV_HEADS)
    def _(j):
        @pl.when(j < KV_HEADS - 1)
        def _():
            service(q_item(j + 1))

        finish(q_item(j))
        queries = jnp.dot(
            normed[MEM:, :], all_q[:, lanes(j, span)], preferred_element_type=f32
        ).astype(bf16)
        key, value = keys[j], values[j]
        pulled = dmixed[j]
        dkey = jnp.zeros(key.shape, f32)
        dvalue = jnp.zeros(value.shape, f32)
        dquery = []
        for h in range(GROUP):
            at = slice(h * HEAD, (h + 1) * HEAD)
            query, dhead = queries[:, at], pulled[:, at]
            scores = lax.dot_general(key, query, NT, preferred_element_type=f32)
            scores = scores * HEAD ** (-0.5) + bias[...]
            raised = jnp.exp(scores - jnp.max(scores, axis=0, keepdims=True))
            probs = raised * (1.0 / jnp.sum(raised, axis=0, keepdims=True))
            dprobs = lax.dot_general(value, dhead, NT, preferred_element_type=f32)
            dprobs = dprobs.astype(bf16).astype(f32)
            drop = jnp.sum(probs * dprobs, axis=0, keepdims=True)
            dscores = (probs * (dprobs - drop) * HEAD ** (-0.5)).astype(bf16)
            dvalue += jnp.dot(probs.astype(bf16), dhead, preferred_element_type=f32)
            dkey += jnp.dot(dscores, query, preferred_element_type=f32)
            dquery.append(lax.dot_general(key, dscores, TN, preferred_element_type=f32))
        dkeys[j] = dkey.astype(bf16)
        dvalues[j] = dvalue.astype(bf16)
        dq[:, lanes(j, span)] = jnp.concatenate(dquery, axis=0).T.astype(bf16)

    dkv = jnp.concatenate(
        [dkeys[h] for h in range(KV_HEADS)] + [dvalues[h] for h in range(KV_HEADS)], axis=1
    )
    tile = 256

    @pl.loop(0, width // tile)
    def _(t):
        at = lanes(t, tile)
        both = lax.dot_general(dkv, all_kv[at, :], NT, preferred_element_type=f32).astype(bf16)
        ones = lax.dot_general(dq[...], all_q[at, :], NT, preferred_element_type=f32).astype(bf16)
        dnormed[:MEM, at] = both[:MEM]
        dnormed[MEM:, at] = (both[MEM:].astype(f32) + ones.astype(f32)).astype(bf16)

    def pull_rows(from_ref, to_ref, from_row, extra):
        @pl.loop(0, from_ref.shape[0] // strip)
        def _(r):
            here = lanes(r, strip)
            there = pl.ds(pl.multiple_of(from_row + r * strip, strip), strip)
            x = from_ref[here, :].astype(f32)
            scale = scales[there, :]
            grown = dnormed[there, :].astype(f32) * gain[...]
            total = jnp.sum(grown * x, axis=-1, keepdims=True)
            dx = grown * scale - x * (total * scale * scale * scale * (1.0 / width))
            if extra is not None:
                dx = dx.astype(bf16).astype(f32) + extra[here, :].astype(f32)
            to_ref[here, :] = dx.astype(bf16)

    pull_rows(memory, grad_memory, 0, None)
    pull_rows(rows_in, grad_rows, MEM, upstream)

    @pl.loop(0, n)
    def _(shard):
        @pl.when(shard < s)
        def _():
            for d in range(1, sections):
                write_peer(shard, d, c).wait_send()

        @pl.when((shard <= s) & (s < n - 1))
        def _():
            write_up(shard).wait_send()

    drain(kv_item)
    drain(o_item)

    @pl.loop(0, CHUNKS)
    def _(j):
        drain(q_item(j))


def per_device(
    n,
    groups,
    sections,
    writes,
    layer_inputs,
    upstream,
    pattern,
    w_q,
    w_kv,
    w_o,
    norm_gain,
    gate_weight,
    gate_bias,
):
    count, width = layer_inputs.shape[2:]
    total = MEM + count
    span = HEADS * HEAD // CHUNKS
    anywhere = pl.BlockSpec(memory_space=pl.ANY)
    near = pl.BlockSpec(memory_space=pltpu.VMEM)
    dma = pltpu.SemaphoreType.DMA
    bf16, f32 = jnp.bfloat16, jnp.float32
    items = 2 + CHUNKS
    grads = pl.pallas_call(
        functools.partial(layer_kernel, n, groups, sections),
        out_shape=[
            jax.ShapeDtypeStruct((count, width), bf16),
            jax.ShapeDtypeStruct((MEM, width), bf16),
        ],
        in_specs=[pl.BlockSpec(memory_space=pltpu.SMEM), anywhere, near, near, near, near, near]
        + [anywhere] * 3,
        out_specs=[near, near],
        scratch_shapes=[
            pltpu.VMEM((n, MEM, width), bf16),
            pltpu.VMEM((width, w_kv.shape[2]), bf16),
            pltpu.VMEM((width, HEADS * HEAD), bf16),
            pltpu.VMEM((HEADS * HEAD, width), bf16),
            pltpu.VMEM((total, width), bf16),
            pltpu.VMEM((total, 1), f32),
            pltpu.VMEM((MEM, width), bf16),
            pltpu.VMEM((MEM, width), f32),
            pltpu.VMEM((3, width, HEADS), bf16),
            pltpu.VMEM((KV_HEADS, total, HEAD), bf16),
            pltpu.VMEM((KV_HEADS, total, HEAD), bf16),
            pltpu.VMEM((total, count), f32),
            pltpu.VMEM((KV_HEADS, count, span), bf16),
            pltpu.VMEM((count, HEADS * HEAD), bf16),
            pltpu.VMEM((KV_HEADS, total, HEAD), bf16),
            pltpu.VMEM((KV_HEADS, total, HEAD), bf16),
            pltpu.VMEM((total, width), bf16),
            dma((items, n)),
            dma((items, n)),
            dma((items, n)),
            dma((items, n, groups)),
            dma((items, n, groups)),
            dma((n,)),
            dma((n,)),
            dma((n, sections)),
            dma((n, sections)),
            dma((3,)),
        ],
        compiler_params=pltpu.CompilerParams(
            collective_id=0, has_side_effects=True, vmem_limit_bytes=56 * 1024 * 1024
        ),
    )(
        pattern[0],
        writes[0],
        layer_inputs[0, 0],
        upstream[0, 0],
        norm_gain,
        gate_weight[0],
        gate_bias,
        w_kv[0],
        w_q[0],
        w_o[0],
    )
    return (grads[0][None, None], grads[1][None, None])


def solution(mesh):
    placed = (
        P(("groups", "seg"), None, "section"),
        P("section", ("groups", "seg"), None, None),
        P("section", ("groups", "seg"), None, None),
        P(("groups", "seg"), None, None),
        P("section", "seg", None),
        P("section", "seg", None),
        P("section", "seg", None),
        P("section", None),
        P("section", None, None),
        P("section", None),
    )
    sizes = (mesh.shape["seg"], mesh.shape["groups"], mesh.shape["section"])
    return jax.shard_map(
        functools.partial(per_device, *sizes),
        mesh=mesh,
        in_specs=placed,
        out_specs=(
            P("section", ("groups", "seg"), None, None),
            P("section", ("groups", "seg"), None, None),
        ),
        check_vma=False,
    )
```

```python
import functools

import jax
import jax.numpy as jnp
from jax import lax
from jax.experimental import pallas as pl
from jax.experimental.pallas import tpu as pltpu
from jax.sharding import PartitionSpec as P

HEADS = 16
KV_HEADS = 4
HEAD = 64
BLK = 128
MEM = 128


epsilon = 1e-05
masked_score = -1e30
GROUP = HEADS // KV_HEADS
NT = (((1,), (1,)), ((), ()))
TN = (((0,), (0,)), ((), ()))
CHUNKS = KV_HEADS
PAIR = 2
OUTS = 2


def layer_kernel(
    n,
    groups,
    sections,
    pattern,
    writes,
    rows_in,
    upstream,
    gain,
    gate,
    gate_bias,
    w_kv,
    w_q,
    w_o,
    grad_rows,
    grad_memory,
    all_writes,
    all_kv,
    all_q,
    all_o,
    normed,
    scales,
    memory,
    state,
    gates,
    keys,
    values,
    bias,
    dmixed,
    dq,
    dkeys,
    dvalues,
    dnormed,
    *sems,
):
    up_sem, down_sem, far_up_sem, far_down_sem, zrecv, ysend, yrecv = sems[:7]
    wsend, wrecv, psend, precv, local = sems[7:]
    g = lax.axis_index("groups")
    s = lax.axis_index("seg")
    c = lax.axis_index("section")
    count, width = rows_in.shape
    wide = writes.shape[1]
    span = all_q.shape[1] // CHUNKS
    f32, bf16 = jnp.float32, jnp.bfloat16

    def lanes(at, size):
        return pl.ds(pl.multiple_of(at * size, size), size)

    mine = lanes(c, wide)
    weights = ((w_kv, all_kv), (w_o, all_o), (w_q, all_q))

    barrier = pltpu.get_barrier_semaphore()

    def greet(where):
        pl.semaphore_signal(
            barrier, inc=1, device_id=where, device_id_type=pl.DeviceIdType.MESH
        )

    @pl.when(s > 0)
    def _():
        greet((g, s - 1, c))

    @pl.when(s < n - 1)
    def _():
        greet((g, s + 1, c))

    @pl.when(s > 1)
    def _():
        greet((g, s - 2, c))

    @pl.when(s < n - 2)
    def _():
        greet((g, s + 2, c))

    for d in range(1, groups):
        greet(((g + d) % groups, s, c))
    for d in range(1, sections):
        greet((g, s, (c + d) % sections))

    beside = (s + n - 1) // n + (2 * n - 2 - s) // n + (s + n - 2) // n + (2 * n - 3 - s) // n
    pl.semaphore_wait(barrier, beside + groups + sections - 2)

    def remote(src, dst, send, recv, where):
        return pltpu.make_async_remote_copy(
            src_ref=src,
            dst_ref=dst,
            send_sem=send,
            recv_sem=recv,
            device_id=where,
            device_id_type=pl.DeviceIdType.MESH,
        )

    bases = (0, PAIR, PAIR + OUTS)
    widths = (all_kv.shape[1] // PAIR, width // OUTS, span)

    def spot(item, shard, part):
        w, chunk = item
        half = weights[w][0].shape[0] // groups
        rows = pl.ds(pl.multiple_of((shard * groups + part) * half, half), half)
        return weights[w][1].at[rows, lanes(chunk, widths[w])]

    def source(item):
        w, chunk = item
        src = weights[w][0]
        return src.at[lanes(g, src.shape[0] // groups), lanes(chunk, widths[w])]

    def index(item):
        return bases[item[0]] + item[1]

    def along(item, shard, sems, step, own=False):
        i, there = index(item), spot(item, shard, g)
        src = source(item) if own else there
        return remote(src, there, sems.at[i, shard], zrecv.at[i, shard], (g, s + step, c))

    def up(item, shard, own=False):
        return along(item, shard, up_sem, 1, own)

    def down(item, shard, own=False):
        return along(item, shard, down_sem, -1, own)

    def far_up(item):
        return along(item, s, far_up_sem, 2, True)

    def far_down(item):
        return along(item, s, far_down_sem, -2, True)

    def across(item, shard, d, part):
        i, there = index(item), spot(item, shard, part)
        return remote(
            there, there, ysend.at[i, shard, d], yrecv.at[i, shard, d], ((g + d) % groups, s, c)
        )

    def write_up(shard, own=False):
        there = all_writes.at[shard, :, mine]
        return remote(
            writes if own else there, there, wsend.at[shard], wrecv.at[shard], (g, s + 1, c)
        )

    def write_peer(shard, d, origin):
        there = all_writes.at[shard, :, lanes(origin, wide)]
        return remote(
            there, there, psend.at[shard, d], precv.at[shard, d], (g, s, (c + d) % sections)
        )

    def own_copy(w):
        src, dst = weights[w]
        return pltpu.make_async_copy(src, dst.at[lanes(s, src.shape[0]), :], local.at[w])

    def start_own(item):
        @pl.when(s < n - 2)
        def _():
            far_up(item).start()

        @pl.when(s > 1)
        def _():
            far_down(item).start()

        @pl.when(s < n - 1)
        def _():
            up(item, s, True).start()

        @pl.when(s > 0)
        def _():
            down(item, s, True).start()

    def service(item):
        @pl.loop(1, n)
        def _(k):
            @pl.when(s - k >= 0)
            def _():
                up(item, s - k).wait_recv()

                @pl.when((k > 1) & (s < n - 1))
                def _():
                    up(item, s - k).start()

                for d in range(1, groups):
                    across(item, s - k, d, g).start()

            @pl.when(s + k < n)
            def _():
                down(item, s + k).wait_recv()

                @pl.when((k > 1) & (s > 0))
                def _():
                    down(item, s + k).start()

                for d in range(1, groups):
                    across(item, s + k, d, g).start()

    def finish(item):
        @pl.loop(0, n)
        def _(shard):
            @pl.when(shard != s)
            def _():
                for d in range(1, groups):
                    across(item, shard, d, (g + groups - d) % groups).wait_recv()

    def drain(item):
        @pl.loop(0, n)
        def _(shard):
            @pl.when(shard != s)
            def _():
                for d in range(1, groups):
                    across(item, shard, d, g).wait_send()

            @pl.when((shard <= s) & (shard != s - 1) & (s < n - 1))
            def _():
                up(item, shard).wait_send()

            @pl.when((shard >= s) & (shard != s + 1) & (s > 0))
            def _():
                down(item, shard).wait_send()

        @pl.when(s < n - 2)
        def _():
            far_up(item).wait_send()

        @pl.when(s > 1)
        def _():
            far_down(item).wait_send()

    def kv_item(chunk):
        return (0, chunk)

    def o_item(chunk):
        return (1, chunk)

    def q_item(chunk):
        return (2, chunk)

    @pl.when(s < n - 1)
    def _():
        write_up(s, True).start()

    start_own(kv_item(0))
    start_own(kv_item(1))

    strip = 32

    def norm_rows(from_ref, to_row):
        @pl.loop(0, from_ref.shape[0] // strip)
        def _(r):
            x = from_ref[lanes(r, strip), :].astype(f32)
            scale = lax.rsqrt(jnp.mean(x * x, axis=-1, keepdims=True) + epsilon)
            to = pl.ds(pl.multiple_of(to_row + r * strip, strip), strip)
            normed[to, :] = (x * scale * gain[...]).astype(bf16)
            scales[to, :] = scale

    norm_rows(rows_in, MEM)
    start_own(o_item(0))
    for w in range(3):
        own_copy(w).start()

    whole_gate = gate[...]
    high = whole_gate.astype(bf16)
    rest = whole_gate - high.astype(f32)
    middle = rest.astype(bf16)
    gates[0] = high
    gates[1] = middle
    gates[2] = (rest - middle.astype(f32)).astype(bf16)

    keyed = lax.broadcasted_iota(jnp.int32, (BLK, BLK), 0)
    asked = lax.broadcasted_iota(jnp.int32, (BLK, BLK), 1)
    blocks = count // BLK
    for b in range(blocks):
        to = slice(b * BLK, (b + 1) * BLK)
        seen = jnp.where(pattern[b, 0] > 0, 0.0, masked_score)
        bias[:MEM, to] = jnp.full((MEM, BLK), seen, f32)
        for e in range(blocks):
            where = slice(MEM + e * BLK, MEM + (e + 1) * BLK)
            if e == b:
                bias[where, to] = jnp.where(keyed <= asked, 0.0, masked_score).astype(f32)
            elif e < b:
                seen = jnp.where(pattern[b, 1 + e] > 0, 0.0, masked_score)
                bias[where, to] = jnp.full((BLK, BLK), seen, f32)
            else:
                bias[where, to] = jnp.full((BLK, BLK), masked_score, f32)

    @pl.loop(1, n)
    def _(k):
        @pl.when(s - k >= 0)
        def _():
            write_up(s - k).wait_recv()

            @pl.when(s < n - 1)
            def _():
                write_up(s - k).start()

            for d in range(1, sections):
                write_peer(s - k, d, c).start()

    service(kv_item(0))
    start_own(o_item(1))
    service(kv_item(1))
    start_own(q_item(0))

    state[...] = jnp.zeros_like(state)
    cut = width // HEADS

    @pl.loop(0, n)
    def _(k):
        @pl.when(k < s)
        def _():
            for d in range(1, sections):
                write_peer(k, d, (c + sections - d) % sections).wait_recv()
            w = all_writes[k]
            logits = sum(
                lax.dot_general(w, gates[p], NT, preferred_element_type=f32) for p in range(3)
            )
            keep = jax.nn.sigmoid(logits + gate_bias[...])
            for h in range(HEADS):
                at = slice(h * cut, (h + 1) * cut)
                share = keep[:, h : h + 1]
                state[:, at] = share * state[:, at] + (1.0 - share) * w[:, at].astype(f32)

    memory[...] = state[...].astype(bf16)
    norm_rows(memory, 0)

    service(o_item(0))
    start_own(q_item(1))

    own_copy(0).wait()
    finish(kv_item(0))
    finish(kv_item(1))
    for kind, to in ((0, keys), (1, values)):
        part = jnp.dot(
            normed[...], all_kv[:, kind * span : (kind + 1) * span], preferred_element_type=f32
        ).astype(bf16)
        for h in range(KV_HEADS):
            to[h] = part[:, h * HEAD : (h + 1) * HEAD]

    service(o_item(1))
    start_own(q_item(2))
    start_own(q_item(3))
    service(q_item(0))

    own_copy(1).wait()
    finish(o_item(0))
    finish(o_item(1))

    @pl.loop(0, KV_HEADS)
    def _(j):
        dmixed[j] = lax.dot_general(
            upstream[...], all_o[lanes(j, span), :], NT, preferred_element_type=f32
        ).astype(bf16)

    own_copy(2).wait()

    @pl.loop(0, KV_HEADS)
    def _(j):
        @pl.when(j < KV_HEADS - 1)
        def _():
            service(q_item(j + 1))

        finish(q_item(j))
        queries = jnp.dot(
            normed[MEM:, :], all_q[:, lanes(j, span)], preferred_element_type=f32
        ).astype(bf16)
        key, value = keys[j], values[j]
        pulled = dmixed[j]
        dkey = jnp.zeros(key.shape, f32)
        dvalue = jnp.zeros(value.shape, f32)
        dquery = []
        for h in range(GROUP):
            at = slice(h * HEAD, (h + 1) * HEAD)
            query, dhead = queries[:, at], pulled[:, at]
            scores = lax.dot_general(key, query, NT, preferred_element_type=f32)
            scores = scores * HEAD ** (-0.5) + bias[...]
            raised = jnp.exp(scores - jnp.max(scores, axis=0, keepdims=True))
            probs = raised * (1.0 / jnp.sum(raised, axis=0, keepdims=True))
            dprobs = lax.dot_general(value, dhead, NT, preferred_element_type=f32)
            dprobs = dprobs.astype(bf16).astype(f32)
            drop = jnp.sum(probs * dprobs, axis=0, keepdims=True)
            dscores = (probs * (dprobs - drop) * HEAD ** (-0.5)).astype(bf16)
            dvalue += jnp.dot(probs.astype(bf16), dhead, preferred_element_type=f32)
            dkey += jnp.dot(dscores, query, preferred_element_type=f32)
            dquery.append(lax.dot_general(key, dscores, TN, preferred_element_type=f32))
        dkeys[j] = dkey.astype(bf16)
        dvalues[j] = dvalue.astype(bf16)
        dq[:, lanes(j, span)] = jnp.concatenate(dquery, axis=0).T.astype(bf16)

    dkv = jnp.concatenate(
        [dkeys[h] for h in range(KV_HEADS)] + [dvalues[h] for h in range(KV_HEADS)], axis=1
    )
    tile = 256

    @pl.loop(0, width // tile)
    def _(t):
        at = lanes(t, tile)
        both = lax.dot_general(dkv, all_kv[at, :], NT, preferred_element_type=f32).astype(bf16)
        ones = lax.dot_general(dq[...], all_q[at, :], NT, preferred_element_type=f32).astype(bf16)
        dnormed[:MEM, at] = both[:MEM]
        dnormed[MEM:, at] = (both[MEM:].astype(f32) + ones.astype(f32)).astype(bf16)

    def pull_rows(from_ref, to_ref, from_row, extra):
        @pl.loop(0, from_ref.shape[0] // strip)
        def _(r):
            here = lanes(r, strip)
            there = pl.ds(pl.multiple_of(from_row + r * strip, strip), strip)
            x = from_ref[here, :].astype(f32)
            scale = scales[there, :]
            grown = dnormed[there, :].astype(f32) * gain[...]
            total = jnp.sum(grown * x, axis=-1, keepdims=True)
            dx = grown * scale - x * (total * scale * scale * scale * (1.0 / width))
            if extra is not None:
                dx = dx.astype(bf16).astype(f32) + extra[here, :].astype(f32)
            to_ref[here, :] = dx.astype(bf16)

    pull_rows(memory, grad_memory, 0, None)
    pull_rows(rows_in, grad_rows, MEM, upstream)

    @pl.loop(0, n)
    def _(shard):
        @pl.when(shard < s)
        def _():
            for d in range(1, sections):
                write_peer(shard, d, c).wait_send()

        @pl.when((shard <= s) & (s < n - 1))
        def _():
            write_up(shard).wait_send()

    @pl.loop(0, PAIR)
    def _(j):
        drain(kv_item(j))

    @pl.loop(0, OUTS)
    def _(j):
        drain(o_item(j))

    @pl.loop(0, CHUNKS)
    def _(j):
        drain(q_item(j))


def per_device(
    n,
    groups,
    sections,
    writes,
    layer_inputs,
    upstream,
    pattern,
    w_q,
    w_kv,
    w_o,
    norm_gain,
    gate_weight,
    gate_bias,
):
    count, width = layer_inputs.shape[2:]
    total = MEM + count
    span = HEADS * HEAD // CHUNKS
    anywhere = pl.BlockSpec(memory_space=pl.ANY)
    near = pl.BlockSpec(memory_space=pltpu.VMEM)
    dma = pltpu.SemaphoreType.DMA
    bf16, f32 = jnp.bfloat16, jnp.float32
    items = PAIR + OUTS + CHUNKS
    grads = pl.pallas_call(
        functools.partial(layer_kernel, n, groups, sections),
        out_shape=[
            jax.ShapeDtypeStruct((count, width), bf16),
            jax.ShapeDtypeStruct((MEM, width), bf16),
        ],
        in_specs=[pl.BlockSpec(memory_space=pltpu.SMEM), anywhere, near, near, near, near, near]
        + [anywhere] * 3,
        out_specs=[near, near],
        scratch_shapes=[
            pltpu.VMEM((n, MEM, width), bf16),
            pltpu.VMEM((width, w_kv.shape[2]), bf16),
            pltpu.VMEM((width, HEADS * HEAD), bf16),
            pltpu.VMEM((HEADS * HEAD, width), bf16),
            pltpu.VMEM((total, width), bf16),
            pltpu.VMEM((total, 1), f32),
            pltpu.VMEM((MEM, width), bf16),
            pltpu.VMEM((MEM, width), f32),
            pltpu.VMEM((3, HEADS, width), bf16),
            pltpu.VMEM((KV_HEADS, total, HEAD), bf16),
            pltpu.VMEM((KV_HEADS, total, HEAD), bf16),
            pltpu.VMEM((total, count), f32),
            pltpu.VMEM((KV_HEADS, count, span), bf16),
            pltpu.VMEM((count, HEADS * HEAD), bf16),
            pltpu.VMEM((KV_HEADS, total, HEAD), bf16),
            pltpu.VMEM((KV_HEADS, total, HEAD), bf16),
            pltpu.VMEM((total, width), bf16),
            dma((items, n)),
            dma((items, n)),
            dma((items, n)),
            dma((items, n)),
            dma((items, n)),
            dma((items, n, groups)),
            dma((items, n, groups)),
            dma((n,)),
            dma((n,)),
            dma((n, sections)),
            dma((n, sections)),
            dma((3,)),
        ],
        compiler_params=pltpu.CompilerParams(
            collective_id=0, has_side_effects=True, vmem_limit_bytes=56 * 1024 * 1024
        ),
    )(
        pattern[0],
        writes[0],
        layer_inputs[0, 0],
        upstream[0, 0],
        norm_gain,
        gate_weight[0].T,
        gate_bias,
        w_kv[0],
        w_q[0],
        w_o[0],
    )
    return (grads[0][None, None], grads[1][None, None])


def solution(mesh):
    placed = (
        P(("groups", "seg"), None, "section"),
        P("section", ("groups", "seg"), None, None),
        P("section", ("groups", "seg"), None, None),
        P(("groups", "seg"), None, None),
        P("section", "seg", None),
        P("section", "seg", None),
        P("section", "seg", None),
        P("section", None),
        P("section", None, None),
        P("section", None),
    )
    sizes = (mesh.shape["seg"], mesh.shape["groups"], mesh.shape["section"])
    return jax.shard_map(
        functools.partial(per_device, *sizes),
        mesh=mesh,
        in_specs=placed,
        out_specs=(
            P("section", ("groups", "seg"), None, None),
            P("section", ("groups", "seg"), None, None),
        ),
        check_vma=False,
    )
```

```python
import functools

import jax
import jax.numpy as jnp
from jax import lax
from jax.experimental import pallas as pl
from jax.experimental.pallas import tpu as pltpu
from jax.sharding import PartitionSpec as P

HEADS = 16
KV_HEADS = 4
HEAD = 64
BLK = 128
MEM = 128


epsilon = 1e-05
masked_score = -1e30
GROUP = HEADS // KV_HEADS
NT = (((1,), (1,)), ((), ()))
TN = (((0,), (0,)), ((), ()))
CHUNKS = KV_HEADS


def layer_kernel(
    n,
    groups,
    sections,
    pattern,
    writes,
    rows_in,
    upstream,
    gain,
    gate,
    gate_bias,
    w_kv,
    w_q,
    w_o,
    grad_rows,
    grad_memory,
    all_writes,
    all_kv,
    all_q,
    all_o,
    normed,
    scales,
    memory,
    state,
    gates,
    keys,
    values,
    bias,
    dmixed,
    dq,
    dkeys,
    dvalues,
    dnormed,
    *sems,
):
    up_sem, down_sem, zrecv, ysend, yrecv, wsend, wrecv, psend, precv, local = sems
    g = lax.axis_index("groups")
    s = lax.axis_index("seg")
    c = lax.axis_index("section")
    count, width = rows_in.shape
    wide = writes.shape[1]
    span = all_q.shape[1] // CHUNKS
    f32, bf16 = jnp.float32, jnp.bfloat16

    def lanes(at, size):
        return pl.ds(pl.multiple_of(at * size, size), size)

    mine = lanes(c, wide)
    weights = ((w_kv, all_kv), (w_o, all_o), (w_q, all_q))

    barrier = pltpu.get_barrier_semaphore()

    def greet(where):
        pl.semaphore_signal(
            barrier, inc=1, device_id=where, device_id_type=pl.DeviceIdType.MESH
        )

    @pl.when(s > 0)
    def _():
        greet((g, s - 1, c))

    @pl.when(s < n - 1)
    def _():
        greet((g, s + 1, c))

    for d in range(1, groups):
        greet(((g + d) % groups, s, c))
    for d in range(1, sections):
        greet((g, s, (c + d) % sections))

    beside = (s + n - 1) // n + (2 * n - 2 - s) // n
    pl.semaphore_wait(barrier, beside + groups + sections - 2)

    def remote(src, dst, send, recv, where):
        return pltpu.make_async_remote_copy(
            src_ref=src,
            dst_ref=dst,
            send_sem=send,
            recv_sem=recv,
            device_id=where,
            device_id_type=pl.DeviceIdType.MESH,
        )

    def spot(item, shard, part):
        w, chunk = item
        src, dst = weights[w]
        half = src.shape[0] // groups
        rows = pl.ds(pl.multiple_of((shard * groups + part) * half, half), half)
        return dst.at[rows, :] if chunk is None else dst.at[rows, lanes(chunk, span)]

    def source(item):
        w, chunk = item
        src, _ = weights[w]
        half = src.shape[0] // groups
        rows = lanes(g, half)
        return src.at[rows, :] if chunk is None else src.at[rows, lanes(chunk, span)]

    def index(item):
        w, chunk = item
        return w if chunk is None else w + chunk

    def up(item, shard, own=False):
        i, there = index(item), spot(item, shard, g)
        src = source(item) if own else there
        return remote(src, there, up_sem.at[i, shard], zrecv.at[i, shard], (g, s + 1, c))

    def down(item, shard, own=False):
        i, there = index(item), spot(item, shard, g)
        src = source(item) if own else there
        return remote(src, there, down_sem.at[i, shard], zrecv.at[i, shard], (g, s - 1, c))

    def across(item, shard, d, part):
        i, there = index(item), spot(item, shard, part)
        return remote(
            there, there, ysend.at[i, shard, d], yrecv.at[i, shard, d], ((g + d) % groups, s, c)
        )

    def write_up(shard, own=False):
        there = all_writes.at[shard, :, mine]
        return remote(
            writes if own else there, there, wsend.at[shard], wrecv.at[shard], (g, s + 1, c)
        )

    def write_peer(shard, d, origin):
        there = all_writes.at[shard, :, lanes(origin, wide)]
        return remote(
            there, there, psend.at[shard, d], precv.at[shard, d], (g, s, (c + d) % sections)
        )

    def own_copy(w):
        src, dst = weights[w]
        return pltpu.make_async_copy(src, dst.at[lanes(s, src.shape[0]), :], local.at[w])

    def start_own(item):
        @pl.when(s < n - 1)
        def _():
            up(item, s, True).start()

        @pl.when(s > 0)
        def _():
            down(item, s, True).start()

    def service(item):
        @pl.loop(1, n)
        def _(k):
            @pl.when(s - k >= 0)
            def _():
                up(item, s - k).wait_recv()

                @pl.when(s < n - 1)
                def _():
                    up(item, s - k).start()

                for d in range(1, groups):
                    across(item, s - k, d, g).start()

            @pl.when(s + k < n)
            def _():
                down(item, s + k).wait_recv()

                @pl.when(s > 0)
                def _():
                    down(item, s + k).start()

                for d in range(1, groups):
                    across(item, s + k, d, g).start()

    def finish(item):
        @pl.loop(0, n)
        def _(shard):
            @pl.when(shard != s)
            def _():
                for d in range(1, groups):
                    across(item, shard, d, (g + groups - d) % groups).wait_recv()

    def drain(item):
        @pl.loop(0, n)
        def _(shard):
            @pl.when(shard != s)
            def _():
                for d in range(1, groups):
                    across(item, shard, d, g).wait_send()

            @pl.when((shard <= s) & (s < n - 1))
            def _():
                up(item, shard).wait_send()

            @pl.when((shard >= s) & (s > 0))
            def _():
                down(item, shard).wait_send()

    kv_item, o_item = (0, None), (1, None)

    def q_item(chunk):
        return (2, chunk)

    @pl.when(s < n - 1)
    def _():
        write_up(s, True).start()

    start_own(kv_item)

    strip = 32

    def norm_rows(from_ref, to_row):
        @pl.loop(0, from_ref.shape[0] // strip)
        def _(r):
            x = from_ref[lanes(r, strip), :].astype(f32)
            scale = lax.rsqrt(jnp.mean(x * x, axis=-1, keepdims=True) + epsilon)
            to = pl.ds(pl.multiple_of(to_row + r * strip, strip), strip)
            normed[to, :] = (x * scale * gain[...]).astype(bf16)
            scales[to, :] = scale

    norm_rows(rows_in, MEM)
    start_own(o_item)
    for w in range(3):
        own_copy(w).start()

    whole_gate = gate[...]
    high = whole_gate.astype(bf16)
    rest = whole_gate - high.astype(f32)
    middle = rest.astype(bf16)
    gates[0] = high
    gates[1] = middle
    gates[2] = (rest - middle.astype(f32)).astype(bf16)

    keyed = lax.broadcasted_iota(jnp.int32, (BLK, BLK), 0)
    asked = lax.broadcasted_iota(jnp.int32, (BLK, BLK), 1)
    blocks = count // BLK
    for b in range(blocks):
        to = slice(b * BLK, (b + 1) * BLK)
        seen = jnp.where(pattern[b, 0] > 0, 0.0, masked_score)
        bias[:MEM, to] = jnp.full((MEM, BLK), seen, f32)
        for e in range(blocks):
            where = slice(MEM + e * BLK, MEM + (e + 1) * BLK)
            if e == b:
                bias[where, to] = jnp.where(keyed <= asked, 0.0, masked_score).astype(f32)
            elif e < b:
                seen = jnp.where(pattern[b, 1 + e] > 0, 0.0, masked_score)
                bias[where, to] = jnp.full((BLK, BLK), seen, f32)
            else:
                bias[where, to] = jnp.full((BLK, BLK), masked_score, f32)

    @pl.loop(1, n)
    def _(k):
        @pl.when(s - k >= 0)
        def _():
            write_up(s - k).wait_recv()

            @pl.when(s < n - 1)
            def _():
                write_up(s - k).start()

            for d in range(1, sections):
                write_peer(s - k, d, c).start()

    service(kv_item)
    start_own(q_item(0))
    start_own(q_item(1))

    state[...] = jnp.zeros_like(state)
    cut = width // HEADS

    @pl.loop(0, n)
    def _(k):
        @pl.when(k < s)
        def _():
            for d in range(1, sections):
                write_peer(k, d, (c + sections - d) % sections).wait_recv()
            w = all_writes[k]
            logits = sum(
                lax.dot_general(w, gates[p], NT, preferred_element_type=f32) for p in range(3)
            )
            keep = jax.nn.sigmoid(logits + gate_bias[...])
            for h in range(HEADS):
                at = slice(h * cut, (h + 1) * cut)
                share = keep[:, h : h + 1]
                state[:, at] = share * state[:, at] + (1.0 - share) * w[:, at].astype(f32)

    memory[...] = state[...].astype(bf16)
    norm_rows(memory, 0)

    service(o_item)
    start_own(q_item(2))
    start_own(q_item(3))

    own_copy(0).wait()
    finish(kv_item)
    for kind, to in ((0, keys), (1, values)):
        part = jnp.dot(
            normed[...], all_kv[:, kind * span : (kind + 1) * span], preferred_element_type=f32
        ).astype(bf16)
        for h in range(KV_HEADS):
            to[h] = part[:, h * HEAD : (h + 1) * HEAD]

    service(q_item(0))

    own_copy(1).wait()
    finish(o_item)

    @pl.loop(0, KV_HEADS)
    def _(j):
        dmixed[j] = lax.dot_general(
            upstream[...], all_o[lanes(j, span), :], NT, preferred_element_type=f32
        ).astype(bf16)

    own_copy(2).wait()

    @pl.loop(0, KV_HEADS)
    def _(j):
        @pl.when(j < KV_HEADS - 1)
        def _():
            service(q_item(j + 1))

        finish(q_item(j))
        queries = jnp.dot(
            normed[MEM:, :], all_q[:, lanes(j, span)], preferred_element_type=f32
        ).astype(bf16)
        key, value = keys[j], values[j]
        pulled = dmixed[j]
        dkey = jnp.zeros(key.shape, f32)
        dvalue = jnp.zeros(value.shape, f32)
        dquery = []
        for h in range(GROUP):
            at = slice(h * HEAD, (h + 1) * HEAD)
            query, dhead = queries[:, at], pulled[:, at]
            scores = lax.dot_general(key, query, NT, preferred_element_type=f32)
            scores = scores * HEAD ** (-0.5) + bias[...]
            raised = jnp.exp(scores - jnp.max(scores, axis=0, keepdims=True))
            probs = raised * (1.0 / jnp.sum(raised, axis=0, keepdims=True))
            dprobs = lax.dot_general(value, dhead, NT, preferred_element_type=f32)
            dprobs = dprobs.astype(bf16).astype(f32)
            drop = jnp.sum(probs * dprobs, axis=0, keepdims=True)
            dscores = (probs * (dprobs - drop) * HEAD ** (-0.5)).astype(bf16)
            dvalue += jnp.dot(probs.astype(bf16), dhead, preferred_element_type=f32)
            dkey += jnp.dot(dscores, query, preferred_element_type=f32)
            dquery.append(lax.dot_general(key, dscores, TN, preferred_element_type=f32))
        dkeys[j] = dkey.astype(bf16)
        dvalues[j] = dvalue.astype(bf16)
        dq[:, lanes(j, span)] = jnp.concatenate(dquery, axis=0).T.astype(bf16)

    dkv = jnp.concatenate(
        [dkeys[h] for h in range(KV_HEADS)] + [dvalues[h] for h in range(KV_HEADS)], axis=1
    )
    tile = 256

    @pl.loop(0, width // tile)
    def _(t):
        at = lanes(t, tile)
        both = lax.dot_general(dkv, all_kv[at, :], NT, preferred_element_type=f32).astype(bf16)
        ones = lax.dot_general(dq[...], all_q[at, :], NT, preferred_element_type=f32).astype(bf16)
        dnormed[:MEM, at] = both[:MEM]
        dnormed[MEM:, at] = (both[MEM:].astype(f32) + ones.astype(f32)).astype(bf16)

    def pull_rows(from_ref, to_ref, from_row):
        @pl.loop(0, from_ref.shape[0] // strip)
        def _(r):
            here = lanes(r, strip)
            there = pl.ds(pl.multiple_of(from_row + r * strip, strip), strip)
            x = from_ref[here, :].astype(f32)
            scale = scales[there, :]
            grown = dnormed[there, :].astype(f32) * gain[...]
            total = jnp.sum(grown * x, axis=-1, keepdims=True)
            dx = grown * scale - x * (total * scale * scale * scale * (1.0 / width))
            to_ref[here, :] = dx.astype(bf16)

    pull_rows(memory, grad_memory, 0)
    pull_rows(rows_in, grad_rows, MEM)

    @pl.loop(0, n)
    def _(shard):
        @pl.when(shard < s)
        def _():
            for d in range(1, sections):
                write_peer(shard, d, c).wait_send()

        @pl.when((shard <= s) & (s < n - 1))
        def _():
            write_up(shard).wait_send()

    drain(kv_item)
    drain(o_item)

    @pl.loop(0, CHUNKS)
    def _(j):
        drain(q_item(j))


def per_device(
    n,
    groups,
    sections,
    writes,
    layer_inputs,
    upstream,
    pattern,
    w_q,
    w_kv,
    w_o,
    norm_gain,
    gate_weight,
    gate_bias,
):
    count, width = layer_inputs.shape[2:]
    total = MEM + count
    span = HEADS * HEAD // CHUNKS
    anywhere = pl.BlockSpec(memory_space=pl.ANY)
    near = pl.BlockSpec(memory_space=pltpu.VMEM)
    dma = pltpu.SemaphoreType.DMA
    bf16, f32 = jnp.bfloat16, jnp.float32
    items = 2 + CHUNKS
    grads = pl.pallas_call(
        functools.partial(layer_kernel, n, groups, sections),
        out_shape=[
            jax.ShapeDtypeStruct((count, width), bf16),
            jax.ShapeDtypeStruct((MEM, width), bf16),
        ],
        in_specs=[pl.BlockSpec(memory_space=pltpu.SMEM), anywhere, near, near, near, near, near]
        + [anywhere] * 3,
        out_specs=[near, near],
        scratch_shapes=[
            pltpu.VMEM((n, MEM, width), bf16),
            pltpu.VMEM((width, w_kv.shape[2]), bf16),
            pltpu.VMEM((width, HEADS * HEAD), bf16),
            pltpu.VMEM((HEADS * HEAD, width), bf16),
            pltpu.VMEM((total, width), bf16),
            pltpu.VMEM((total, 1), f32),
            pltpu.VMEM((MEM, width), bf16),
            pltpu.VMEM((MEM, width), f32),
            pltpu.VMEM((3, HEADS, width), bf16),
            pltpu.VMEM((KV_HEADS, total, HEAD), bf16),
            pltpu.VMEM((KV_HEADS, total, HEAD), bf16),
            pltpu.VMEM((total, count), f32),
            pltpu.VMEM((KV_HEADS, count, span), bf16),
            pltpu.VMEM((count, HEADS * HEAD), bf16),
            pltpu.VMEM((KV_HEADS, total, HEAD), bf16),
            pltpu.VMEM((KV_HEADS, total, HEAD), bf16),
            pltpu.VMEM((total, width), bf16),
            dma((items, n)),
            dma((items, n)),
            dma((items, n)),
            dma((items, n, groups)),
            dma((items, n, groups)),
            dma((n,)),
            dma((n,)),
            dma((n, sections)),
            dma((n, sections)),
            dma((3,)),
        ],
        compiler_params=pltpu.CompilerParams(
            collective_id=0, has_side_effects=True, vmem_limit_bytes=56 * 1024 * 1024
        ),
    )(
        pattern[0],
        writes[0],
        layer_inputs[0, 0],
        upstream[0, 0],
        norm_gain,
        gate_weight[0].T,
        gate_bias,
        w_kv[0],
        w_q[0],
        w_o[0],
    )
    grad_rows = (grads[0].astype(f32) + upstream[0, 0].astype(f32)).astype(bf16)
    return (grad_rows[None, None], grads[1][None, None])


def solution(mesh):
    placed = (
        P(("groups", "seg"), None, "section"),
        P("section", ("groups", "seg"), None, None),
        P("section", ("groups", "seg"), None, None),
        P(("groups", "seg"), None, None),
        P("section", "seg", None),
        P("section", "seg", None),
        P("section", "seg", None),
        P("section", None),
        P("section", None, None),
        P("section", None),
    )
    sizes = (mesh.shape["seg"], mesh.shape["groups"], mesh.shape["section"])
    return jax.shard_map(
        functools.partial(per_device, *sizes),
        mesh=mesh,
        in_specs=placed,
        out_specs=(
            P("section", ("groups", "seg"), None, None),
            P("section", ("groups", "seg"), None, None),
        ),
        check_vma=False,
    )
```

```python
import functools

import jax
import jax.numpy as jnp
from jax import lax
from jax.experimental import pallas as pl
from jax.experimental.pallas import tpu as pltpu
from jax.sharding import PartitionSpec as P

HEADS = 16
KV_HEADS = 4
HEAD = 64
BLK = 128
MEM = 128


epsilon = 1e-05
masked_score = -1e30
GROUP = HEADS // KV_HEADS
NT = (((1,), (1,)), ((), ()))
TN = (((0,), (0,)), ((), ()))
CHUNKS = KV_HEADS


def layer_kernel(
    n,
    groups,
    sections,
    pattern,
    writes,
    rows_in,
    upstream,
    gain,
    gate,
    gate_bias,
    w_kv,
    w_q,
    w_o,
    grad_rows,
    grad_memory,
    all_writes,
    all_kv,
    all_q,
    all_o,
    normed,
    scales,
    memory,
    state,
    gates,
    keys,
    values,
    bias,
    dmixed,
    dq,
    dkeys,
    dvalues,
    dnormed,
    asking,
    dasking,
    dsums,
    *sems,
):
    up_sem, down_sem, zrecv, ysend, yrecv, wsend, wrecv, psend, precv, local = sems
    g = lax.axis_index("groups")
    s = lax.axis_index("seg")
    c = lax.axis_index("section")
    count, width = rows_in.shape
    wide = writes.shape[1]
    span = all_q.shape[1] // CHUNKS
    f32, bf16 = jnp.float32, jnp.bfloat16

    def lanes(at, size):
        return pl.ds(pl.multiple_of(at * size, size), size)

    mine = lanes(c, wide)
    weights = ((w_kv, all_kv), (w_o, all_o), (w_q, all_q))

    barrier = pltpu.get_barrier_semaphore()

    def greet(where):
        pl.semaphore_signal(
            barrier, inc=1, device_id=where, device_id_type=pl.DeviceIdType.MESH
        )

    @pl.when(s > 0)
    def _():
        greet((g, s - 1, c))

    @pl.when(s < n - 1)
    def _():
        greet((g, s + 1, c))

    for d in range(1, groups):
        greet(((g + d) % groups, s, c))
    for d in range(1, sections):
        greet((g, s, (c + d) % sections))

    beside = (s + n - 1) // n + (2 * n - 2 - s) // n
    pl.semaphore_wait(barrier, beside + groups + sections - 2)

    def remote(src, dst, send, recv, where):
        return pltpu.make_async_remote_copy(
            src_ref=src,
            dst_ref=dst,
            send_sem=send,
            recv_sem=recv,
            device_id=where,
            device_id_type=pl.DeviceIdType.MESH,
        )

    def spot(item, shard, part):
        w, chunk = item
        src, dst = weights[w]
        half = src.shape[0] // groups
        rows = pl.ds(pl.multiple_of((shard * groups + part) * half, half), half)
        return dst.at[rows, :] if chunk is None else dst.at[rows, lanes(chunk, span)]

    def source(item):
        w, chunk = item
        src, _ = weights[w]
        half = src.shape[0] // groups
        rows = lanes(g, half)
        return src.at[rows, :] if chunk is None else src.at[rows, lanes(chunk, span)]

    def index(item):
        w, chunk = item
        return w if chunk is None else w + chunk

    def up(item, shard, own=False):
        i, there = index(item), spot(item, shard, g)
        src = source(item) if own else there
        return remote(src, there, up_sem.at[i, shard], zrecv.at[i, shard], (g, s + 1, c))

    def down(item, shard, own=False):
        i, there = index(item), spot(item, shard, g)
        src = source(item) if own else there
        return remote(src, there, down_sem.at[i, shard], zrecv.at[i, shard], (g, s - 1, c))

    def across(item, shard, d, part):
        i, there = index(item), spot(item, shard, part)
        return remote(
            there, there, ysend.at[i, shard, d], yrecv.at[i, shard, d], ((g + d) % groups, s, c)
        )

    def write_up(shard, own=False):
        there = all_writes.at[shard, :, mine]
        return remote(
            writes if own else there, there, wsend.at[shard], wrecv.at[shard], (g, s + 1, c)
        )

    def write_peer(shard, d, origin):
        there = all_writes.at[shard, :, lanes(origin, wide)]
        return remote(
            there, there, psend.at[shard, d], precv.at[shard, d], (g, s, (c + d) % sections)
        )

    def own_copy(w):
        src, dst = weights[w]
        return pltpu.make_async_copy(src, dst.at[lanes(s, src.shape[0]), :], local.at[w])

    def start_own(item):
        @pl.when(s < n - 1)
        def _():
            up(item, s, True).start()

        @pl.when(s > 0)
        def _():
            down(item, s, True).start()

    def service(item, first=1, last=n):
        if first >= last:
            return

        @pl.loop(first, last)
        def _(k):
            @pl.when(s - k >= 0)
            def _():
                up(item, s - k).wait_recv()

                @pl.when(s < n - 1)
                def _():
                    up(item, s - k).start()

                for d in range(1, groups):
                    across(item, s - k, d, g).start()

            @pl.when(s + k < n)
            def _():
                down(item, s + k).wait_recv()

                @pl.when(s > 0)
                def _():
                    down(item, s + k).start()

                for d in range(1, groups):
                    across(item, s + k, d, g).start()

    def finish(item):
        @pl.loop(0, n)
        def _(shard):
            @pl.when(shard != s)
            def _():
                for d in range(1, groups):
                    across(item, shard, d, (g + groups - d) % groups).wait_recv()

    def drain(item):
        @pl.loop(0, n)
        def _(shard):
            @pl.when(shard != s)
            def _():
                for d in range(1, groups):
                    across(item, shard, d, g).wait_send()

            @pl.when((shard <= s) & (s < n - 1))
            def _():
                up(item, shard).wait_send()

            @pl.when((shard >= s) & (s > 0))
            def _():
                down(item, shard).wait_send()

    kv_item, o_item = (0, None), (1, None)

    def q_item(chunk):
        return (2, chunk)

    @pl.when(s < n - 1)
    def _():
        write_up(s, True).start()

    start_own(kv_item)

    strip = 32

    def norm_rows(from_ref, to_row):
        @pl.loop(0, from_ref.shape[0] // strip)
        def _(r):
            x = from_ref[lanes(r, strip), :].astype(f32)
            scale = lax.rsqrt(jnp.mean(x * x, axis=-1, keepdims=True) + epsilon)
            to = pl.ds(pl.multiple_of(to_row + r * strip, strip), strip)
            normed[to, :] = (x * scale * gain[...]).astype(bf16)
            scales[to, :] = scale

    norm_rows(rows_in, MEM)
    start_own(o_item)
    for w in range(3):
        own_copy(w).start()

    whole_gate = gate[...]
    high = whole_gate.astype(bf16)
    rest = whole_gate - high.astype(f32)
    middle = rest.astype(bf16)
    gates[0] = high
    gates[1] = middle
    gates[2] = (rest - middle.astype(f32)).astype(bf16)

    keyed = lax.broadcasted_iota(jnp.int32, (BLK, BLK), 0)
    asked = lax.broadcasted_iota(jnp.int32, (BLK, BLK), 1)
    blocks = count // BLK
    for b in range(blocks):
        to = slice(b * BLK, (b + 1) * BLK)
        seen = jnp.where(pattern[b, 0] > 0, 0.0, masked_score)
        bias[:MEM, to] = jnp.full((MEM, BLK), seen, f32)
        for e in range(blocks):
            where = slice(MEM + e * BLK, MEM + (e + 1) * BLK)
            if e == b:
                bias[where, to] = jnp.where(keyed <= asked, 0.0, masked_score).astype(f32)
            elif e < b:
                seen = jnp.where(pattern[b, 1 + e] > 0, 0.0, masked_score)
                bias[where, to] = jnp.full((BLK, BLK), seen, f32)
            else:
                bias[where, to] = jnp.full((BLK, BLK), masked_score, f32)

    @pl.loop(1, n)
    def _(k):
        @pl.when(s - k >= 0)
        def _():
            write_up(s - k).wait_recv()

            @pl.when(s < n - 1)
            def _():
                write_up(s - k).start()

            for d in range(1, sections):
                write_peer(s - k, d, c).start()

    service(kv_item)
    start_own(q_item(0))
    start_own(q_item(1))

    state[...] = jnp.zeros_like(state)
    cut = width // HEADS

    @pl.loop(0, n)
    def _(k):
        @pl.when(k < s)
        def _():
            for d in range(1, sections):
                write_peer(k, d, (c + sections - d) % sections).wait_recv()
            w = all_writes[k]
            logits = sum(
                lax.dot_general(w, gates[p], NT, preferred_element_type=f32) for p in range(3)
            )
            keep = jax.nn.sigmoid(logits + gate_bias[...])
            for h in range(HEADS):
                at = slice(h * cut, (h + 1) * cut)
                share = keep[:, h : h + 1]
                state[:, at] = share * state[:, at] + (1.0 - share) * w[:, at].astype(f32)

    memory[...] = state[...].astype(bf16)
    norm_rows(memory, 0)

    service(o_item)
    start_own(q_item(2))
    start_own(q_item(3))

    own_copy(0).wait()
    finish(kv_item)
    for kind, to in ((0, keys), (1, values)):
        part = jnp.dot(
            normed[...], all_kv[:, kind * span : (kind + 1) * span], preferred_element_type=f32
        ).astype(bf16)
        for h in range(KV_HEADS):
            to[h] = part[:, h * HEAD : (h + 1) * HEAD]

    service(q_item(0))
    service(q_item(1))

    own_copy(1).wait()
    finish(o_item)

    @pl.loop(0, KV_HEADS)
    def _(j):
        dmixed[j] = lax.dot_general(
            upstream[...], all_o[lanes(j, span), :], NT, preferred_element_type=f32
        ).astype(bf16)

    own_copy(2).wait()

    @pl.loop(0, KV_HEADS)
    def _(j):
        finish(q_item(j))
        asking[...] = jnp.dot(
            normed[MEM:, :], all_q[:, lanes(j, span)], preferred_element_type=f32
        ).astype(bf16)
        dsums[...] = jnp.zeros_like(dsums)
        for h in range(GROUP):
            at = slice(h * HEAD, (h + 1) * HEAD)
            key, value = keys[j], values[j]
            query, dhead = asking[:, at], dmixed[j][:, at]
            scores = lax.dot_general(key, query, NT, preferred_element_type=f32)
            scores = scores * HEAD ** (-0.5) + bias[...]
            raised = jnp.exp(scores - jnp.max(scores, axis=0, keepdims=True))
            probs = raised * (1.0 / jnp.sum(raised, axis=0, keepdims=True))
            dprobs = lax.dot_general(value, dhead, NT, preferred_element_type=f32)
            dprobs = dprobs.astype(bf16).astype(f32)
            drop = jnp.sum(probs * dprobs, axis=0, keepdims=True)
            dscores = (probs * (dprobs - drop) * HEAD ** (-0.5)).astype(bf16)
            dsums[0] += jnp.dot(dscores, query, preferred_element_type=f32)
            dsums[1] += jnp.dot(probs.astype(bf16), dhead, preferred_element_type=f32)
            dasking[at, :] = lax.dot_general(key, dscores, TN, preferred_element_type=f32)
            first, last = 1 + h * (n - 1) // GROUP, 1 + (h + 1) * (n - 1) // GROUP
            if first < last:

                @pl.when(j < KV_HEADS - 2)
                def _(first=first, last=last):
                    service(q_item(j + 2), first, last)

        dkeys[j] = dsums[0].astype(bf16)
        dvalues[j] = dsums[1].astype(bf16)
        dq[:, lanes(j, span)] = dasking[...].T.astype(bf16)

    dkv = jnp.concatenate(
        [dkeys[h] for h in range(KV_HEADS)] + [dvalues[h] for h in range(KV_HEADS)], axis=1
    )
    tile = 256

    @pl.loop(0, width // tile)
    def _(t):
        at = lanes(t, tile)
        both = lax.dot_general(dkv, all_kv[at, :], NT, preferred_element_type=f32).astype(bf16)
        ones = lax.dot_general(dq[...], all_q[at, :], NT, preferred_element_type=f32).astype(bf16)
        dnormed[:MEM, at] = both[:MEM]
        dnormed[MEM:, at] = (both[MEM:].astype(f32) + ones.astype(f32)).astype(bf16)

    def pull_rows(from_ref, to_ref, from_row):
        @pl.loop(0, from_ref.shape[0] // strip)
        def _(r):
            here = lanes(r, strip)
            there = pl.ds(pl.multiple_of(from_row + r * strip, strip), strip)
            x = from_ref[here, :].astype(f32)
            scale = scales[there, :]
            grown = dnormed[there, :].astype(f32) * gain[...]
            total = jnp.sum(grown * x, axis=-1, keepdims=True)
            dx = grown * scale - x * (total * scale * scale * scale * (1.0 / width))
            to_ref[here, :] = dx.astype(bf16)

    pull_rows(memory, grad_memory, 0)
    pull_rows(rows_in, grad_rows, MEM)

    @pl.loop(0, n)
    def _(shard):
        @pl.when(shard < s)
        def _():
            for d in range(1, sections):
                write_peer(shard, d, c).wait_send()

        @pl.when((shard <= s) & (s < n - 1))
        def _():
            write_up(shard).wait_send()

    drain(kv_item)
    drain(o_item)

    @pl.loop(0, CHUNKS)
    def _(j):
        drain(q_item(j))


def per_device(
    n,
    groups,
    sections,
    writes,
    layer_inputs,
    upstream,
    pattern,
    w_q,
    w_kv,
    w_o,
    norm_gain,
    gate_weight,
    gate_bias,
):
    count, width = layer_inputs.shape[2:]
    total = MEM + count
    span = HEADS * HEAD // CHUNKS
    anywhere = pl.BlockSpec(memory_space=pl.ANY)
    near = pl.BlockSpec(memory_space=pltpu.VMEM)
    dma = pltpu.SemaphoreType.DMA
    bf16, f32 = jnp.bfloat16, jnp.float32
    items = 2 + CHUNKS
    grads = pl.pallas_call(
        functools.partial(layer_kernel, n, groups, sections),
        out_shape=[
            jax.ShapeDtypeStruct((count, width), bf16),
            jax.ShapeDtypeStruct((MEM, width), bf16),
        ],
        in_specs=[pl.BlockSpec(memory_space=pltpu.SMEM), anywhere, near, near, near, near, near]
        + [anywhere] * 3,
        out_specs=[near, near],
        scratch_shapes=[
            pltpu.VMEM((n, MEM, width), bf16),
            pltpu.VMEM((width, w_kv.shape[2]), bf16),
            pltpu.VMEM((width, HEADS * HEAD), bf16),
            pltpu.VMEM((HEADS * HEAD, width), bf16),
            pltpu.VMEM((total, width), bf16),
            pltpu.VMEM((total, 1), f32),
            pltpu.VMEM((MEM, width), bf16),
            pltpu.VMEM((MEM, width), f32),
            pltpu.VMEM((3, HEADS, width), bf16),
            pltpu.VMEM((KV_HEADS, total, HEAD), bf16),
            pltpu.VMEM((KV_HEADS, total, HEAD), bf16),
            pltpu.VMEM((total, count), f32),
            pltpu.VMEM((KV_HEADS, count, span), bf16),
            pltpu.VMEM((count, HEADS * HEAD), bf16),
            pltpu.VMEM((KV_HEADS, total, HEAD), bf16),
            pltpu.VMEM((KV_HEADS, total, HEAD), bf16),
            pltpu.VMEM((total, width), bf16),
            pltpu.VMEM((count, span), bf16),
            pltpu.VMEM((span, count), f32),
            pltpu.VMEM((2, total, HEAD), f32),
            dma((items, n)),
            dma((items, n)),
            dma((items, n)),
            dma((items, n, groups)),
            dma((items, n, groups)),
            dma((n,)),
            dma((n,)),
            dma((n, sections)),
            dma((n, sections)),
            dma((3,)),
        ],
        compiler_params=pltpu.CompilerParams(
            collective_id=0, has_side_effects=True, vmem_limit_bytes=56 * 1024 * 1024
        ),
    )(
        pattern[0],
        writes[0],
        layer_inputs[0, 0],
        upstream[0, 0],
        norm_gain,
        gate_weight[0].T,
        gate_bias,
        w_kv[0],
        w_q[0],
        w_o[0],
    )
    grad_rows = (grads[0].astype(f32) + upstream[0, 0].astype(f32)).astype(bf16)
    return (grad_rows[None, None], grads[1][None, None])


def solution(mesh):
    placed = (
        P(("groups", "seg"), None, "section"),
        P("section", ("groups", "seg"), None, None),
        P("section", ("groups", "seg"), None, None),
        P(("groups", "seg"), None, None),
        P("section", "seg", None),
        P("section", "seg", None),
        P("section", "seg", None),
        P("section", None),
        P("section", None, None),
        P("section", None),
    )
    sizes = (mesh.shape["seg"], mesh.shape["groups"], mesh.shape["section"])
    return jax.shard_map(
        functools.partial(per_device, *sizes),
        mesh=mesh,
        in_specs=placed,
        out_specs=(
            P("section", ("groups", "seg"), None, None),
            P("section", ("groups", "seg"), None, None),
        ),
        check_vma=False,
    )
```
